32 devices in a mesh: row: 4 (over x, core), col: 8 (over z, y).
Axes of the slice: x: 2, y: 2, z: 4, core: 2. Of those that a mesh axis runs over, the one named last changes fastest.
Arguments:
- object_slices: float32 [4, 2, 1024, 2048], P(None, None, 'row', 'col'), may hold values from -2.5 to 2.5
- probe_wave: float32 [2, 128, 128], replicated, may hold values from -4 to 4
- offsets: int32 [4, 8, 4, 2], P('row', 'col'), may hold values from 0 to 255
- active_flags: int32 [4, 8, 4], P('row', 'col'), may hold values 0 or 1
- intensity: float32 [4, 8, 4, 128, 128], P('row', 'col'), may hold values from 0.1 to 3
Outputs:
- updated_object: float32 [4, 2, 1024, 2048], P(None, None, 'row', 'col')
- updated_probe: float32 [2, 128, 128], replicated
The draws below stay inside these ranges and needn't reach their ends.
Inputs may be any that keep to these rules, and one draw needn't show every extreme that they name: `offsets`: each position's centre lies in its own device's tile; its window may reach into neighbouring tiles, diagonal ones included. `active_flags`: positions with flag 0 contribute nothing.
All inputs are finite; a program needn't handle non-finite values. No bound on the sum of `active_flags` on one device may be relied on, other than what follows from the above.
Results may differ from the reference program's by a relative error of at most 0.00018.
Values sent between devices are 32-bit elements; how exact they have to be, the bound alone decides.
No kernel may reach another device: no remote copies, remote signals or barrier semaphores. Data moves between devices by JAX's collectives and lax.ppermute only.
A program may use at most 64 MiB of HBM per device.

```python
import math
import jax
import jax.numpy as jnp
from jax import lax

SLICES = 4
PROBE = 128
TILE = 256
POS = 4
ROWS = 1024
COLS = 2048
N_ROW = 4
N_COL = 8


def with_ends(array, stream_key, low, largest):
    longest = array.shape.index(max(array.shape))
    spots = []
    for shift in (0, 1):
        where = [jax.random.randint(jax.random.fold_in(stream_key, axis), (), 0, length) for axis, length in enumerate(array.shape)]
        where[longest] = (where[longest] + shift) % array.shape[longest]
        spots.append(tuple(where))
    return array.at[spots[0]].set(low).at[spots[1]].set(largest)


def shard_levels(stream_key, shape, shards, low, largest):
    def one(position, parts):
        steps = jax.random.uniform(jax.random.fold_in(jax.random.fold_in(stream_key, 6), position), (parts,), jnp.float32, low / len(shards), largest / len(shards))
        return jnp.repeat(jnp.exp(steps), shape[position] // parts).reshape((-1,) + (1,) * (len(shape) - position - 1))

    level = one(*shards[0])
    for cut in shards[1:]:
        level = level * one(*cut)
    return level


def centred(rng, shape, deviation, reach, cuts=(), kind=jnp.bfloat16):
    drawn = jax.random.normal(rng, shape, jnp.float32) * deviation
    if len(cuts) > 0:
        drawn = shard_levels(rng, shape, cuts, -0.22, 0.18) * drawn
    return jnp.clip(drawn, min=-reach, max=reach).astype(kind)


def setup_inputs(seed: int = 0) -> dict:
    arg_keys = jax.random.split(jax.random.key(seed), 6)
    object_slices = centred(arg_keys[0], (SLICES, 2, ROWS, COLS), 0.7, 2.5, ((2, 4), (3, 8)), jnp.float32)
    probe_wave = centred(arg_keys[1], (2, PROBE, PROBE), 0.7, 4.0, (), jnp.float32)
    offsets = with_ends(jax.random.randint(arg_keys[2], (N_ROW, N_COL, POS, 2), 0, TILE), jax.random.fold_in(arg_keys[2], 1), 0, TILE - 1).astype(jnp.int32)
    active_flags = with_ends((jax.random.randint(arg_keys[3], (N_ROW, N_COL, POS), 0, 4) < 3).astype(jnp.int32), jax.random.fold_in(arg_keys[3], 1), 0, 1)
    intensity = jnp.clip(jnp.exp(math.log(3.0) - 3.4011974 * jax.random.uniform(arg_keys[4], (N_ROW, N_COL, POS, PROBE, PROBE), jnp.float32) ** shard_levels(arg_keys[4], (N_ROW, N_COL, POS, PROBE, PROBE), ((0, 4), (1, 8)), -0.2, 0.2)), 0.1, 3.0)
    return {"object_slices": object_slices, "probe_wave": probe_wave, "offsets": offsets, "active_flags": active_flags, "intensity": intensity}


fresnel_phase = 40.0
object_step = 0.25

def transfer(extent):
    indices = jnp.arange(extent, dtype=jnp.int32)
    frequency = ((indices + extent // 2) % extent - extent // 2).astype(jnp.float32) / extent
    phase_angle = -jnp.pi * fresnel_phase * (frequency[:, None] ** 2 + frequency[None, :] ** 2)
    return (jnp.cos(phase_angle), jnp.sin(phase_angle))

def position_grads(windows, probe_wave, pattern, flag_value, kernel):
    kernel_c = lax.complex(kernel[0], kernel[1])
    transmit = lax.complex(windows[:, 0], windows[:, 1])
    wavefield = lax.complex(probe_wave[0], probe_wave[1])
    incident = []
    exited = wavefield
    for layer_at in range(SLICES):
        incident.append(wavefield)
        exited = wavefield * transmit[layer_at]
        if layer_at + 1 < SLICES:
            wavefield = jnp.fft.ifft2(kernel_c * jnp.fft.fft2(exited, norm='ortho'), norm='ortho')
    far_field = jnp.fft.fft2(exited, norm='ortho')
    excess = flag_value * (jnp.real(far_field) ** 2 + jnp.imag(far_field) ** 2 - pattern)
    back_field = jnp.fft.ifft2(excess * far_field, norm='ortho')
    gradients = [None] * SLICES
    for layer_at in reversed(range(SLICES)):
        gradients[layer_at] = jnp.conj(incident[layer_at]) * back_field
        back_field = jnp.conj(transmit[layer_at]) * back_field
        if layer_at > 0:
            back_field = jnp.fft.ifft2(jnp.conj(kernel_c) * jnp.fft.fft2(back_field, norm='ortho'), norm='ortho')
    grad_window = jnp.stack([jnp.stack([jnp.real(grad_item), jnp.imag(grad_item)]) for grad_item in gradients])
    grad_wave = jnp.stack([jnp.real(back_field), jnp.imag(back_field)])
    return (grad_window, grad_wave)

def fold_rims(grad_pad, margin):
    inner = grad_pad[:, :, :, margin:-margin]
    inner = inner.at[:, :, :, -margin:].add(grad_pad[:, :, :, :margin])
    inner = inner.at[:, :, :, :margin].add(grad_pad[:, :, :, -margin:])
    folded = inner[:, :, margin:-margin]
    folded = folded.at[:, :, -margin:].add(inner[:, :, :margin])
    folded = folded.at[:, :, :margin].add(inner[:, :, -margin:])
    return folded

def reference(object_slices, probe_wave, offsets, active_flags, intensity):
    margin = PROBE // 2
    padded = jnp.pad(object_slices, ((0, 0), (0, 0), (margin, margin), (margin, margin)), mode='wrap')
    kernel = transfer(PROBE)
    tile_rows = jnp.arange(N_ROW, dtype=jnp.int32)[:, None, None] * TILE
    tile_cols = jnp.arange(N_COL, dtype=jnp.int32)[None, :, None] * TILE
    start_rows = (offsets[..., 0] + tile_rows).reshape(-1).astype(jnp.int32)
    start_cols = (offsets[..., 1] + tile_cols).reshape(-1).astype(jnp.int32)
    flag_list = active_flags.reshape(-1)
    observed = intensity.reshape(-1, PROBE, PROBE)

    def accumulate(running, record):
        grad_pad, grad_probe = running
        top_row, left_col, flag_value, pattern = record
        anchor = jnp.zeros((), jnp.int32)
        begin = (anchor, anchor, top_row, left_col)
        windows = lax.dynamic_slice(padded, begin, (SLICES, 2, PROBE, PROBE))
        grad_window, grad_wave = position_grads(windows, probe_wave, pattern, flag_value.astype(jnp.float32), kernel)
        previous = lax.dynamic_slice(grad_pad, begin, (SLICES, 2, PROBE, PROBE))
        grad_pad = lax.dynamic_update_slice(grad_pad, previous + grad_window, begin)
        return ((grad_pad, grad_probe + grad_wave), None)
    initial = (jnp.zeros_like(padded), jnp.zeros_like(probe_wave))
    (grad_pad, grad_probe), _ = lax.scan(accumulate, initial, (start_rows, start_cols, flag_list, observed))
    object_gradient = fold_rims(grad_pad, margin)
    updated_object = object_slices - object_step * object_gradient
    updated_probe = probe_wave - grad_probe * (1.0 / math.sqrt(POS * N_ROW * N_COL))
    return (updated_object, updated_probe)
```

```python
import functools
import math

import jax
import jax.numpy as jnp
import numpy as np
from jax import lax
from jax.experimental import pallas as pl
from jax.experimental.pallas import tpu as pltpu
from jax.sharding import PartitionSpec as P

fresnel_phase = 40.0
object_step = 0.25
f32 = jnp.float32
bf16 = jnp.bfloat16
VM = pl.BlockSpec(memory_space=pltpu.VMEM)
SM = pl.BlockSpec(memory_space=pltpu.SMEM)
LANES = 128
PARAMS = pltpu.CompilerParams(vmem_limit_bytes=40 << 20)


def split_np(matrix):
    high = matrix.astype(np.float32).astype(jnp.bfloat16)
    low = (matrix - high.astype(np.float64)).astype(np.float32).astype(jnp.bfloat16)
    return high, low


@functools.lru_cache(None)
def tables_np(extent):
    at = np.arange(extent)
    angle = 2.0 * np.pi * (np.outer(at, at) % extent) / extent
    dft = (np.cos(angle) - 1j * np.sin(angle)) / math.sqrt(extent)
    freq = ((at + extent // 2) % extent - extent // 2) / extent
    line = np.exp(-1j * np.pi * fresnel_phase * freq**2)
    prop = (np.conj(dft) * line[None, :]) @ dft
    prop = (prop + prop.T) / 2
    out = []
    for m in (prop, dft):
        right = np.block([[m.real, m.imag], [-m.imag, m.real]])
        left = np.block([[m.real, -m.imag], [m.imag, m.real]])
        out += [*split_np(right), *split_np(left)]
    return np.stack(out)


def halves(x):
    high = x.astype(bf16)
    return high, (x - high.astype(f32)).astype(bf16)


def dot(a, b):
    return jnp.dot(a, b, preferred_element_type=f32)


def times_right(x, high, low):
    xh, xl = halves(x)
    return dot(xh, high) + (dot(xl, high) + dot(xh, low))


def times_left(high, low, x):
    xh, xl = halves(x)
    return dot(high, xh) + (dot(high, xl) + dot(low, xh))


def swapped(x):
    n, m = x.shape[0] // 2, x.shape[1] // 2
    return jnp.concatenate(
        [
            jnp.concatenate([x[:n, :m], x[n:, :m]], axis=1),
            jnp.concatenate([x[:n, m:], x[n:, m:]], axis=1),
        ],
        axis=0,
    )


def sandwich(x, tab, base, conj):
    r, l = (base + 2, base) if conj else (base, base + 2)
    y = times_right(x, tab[r], tab[r + 1])
    z = times_left(tab[l], tab[l + 1], swapped(y))
    return swapped(z)


def cmul(a, b, conj=False):
    n = a.shape[1] // 2
    ar, ai, br, bi = a[:, :n], a[:, n:], b[:, :n], b[:, n:]
    if conj:
        return jnp.concatenate([ar * br + ai * bi, ar * bi - ai * br], axis=1)
    return jnp.concatenate([ar * br - ai * bi, ar * bi + ai * br], axis=1)


def lane_mask(rows):
    return lax.broadcasted_iota(jnp.int32, (rows, LANES), 1)


def parity(axis):
    return lax.rem(lax.axis_index(axis), 2)


def col_place(offs, p, extent):
    first = offs[0, 0, p, 1] - extent // 2
    first = jnp.where(first < 0, first + 3 * LANES, first)
    tile = lax.div(first, LANES)
    shift = lax.rem(first, LANES)
    after = jnp.where(tile == 2, 0, tile + 1)
    return tile, after, shift


def store_by(parity_value, a_ref, b_ref, index, when_even, when_odd):
    @pl.when(parity_value == 0)
    def _():
        a_ref[index] = when_even
        b_ref[index] = when_odd

    @pl.when(parity_value != 0)
    def _():
        a_ref[index] = when_odd
        b_ref[index] = when_even


def pack_kernel(obj, col_a, col_b, row_a, row_b):
    cp, rp = parity("col"), parity("row")
    layers, _, height, width = obj.shape
    half = LANES // 2
    lane = lane_mask(height)
    for k in range(layers):
        right = jnp.where(
            lane < half,
            pltpu.roll(obj[k, 0, :, width - LANES :], half, 1),
            obj[k, 1, :, width - LANES :],
        )
        left = jnp.where(lane < half, obj[k, 0, :, :LANES], pltpu.roll(obj[k, 1, :, :LANES], half, 1))
        store_by(cp, col_a, col_b, k, right, left)
        for q in range(2):
            store_by(rp, row_a, row_b, (k, q), obj[k, q, height - half :], obj[k, q, :half])


def unpack_kernel(col_a, col_b, tile3, corner_a, corner_b):
    cp, rp = parity("col"), parity("row")
    layers, height, _ = col_a.shape
    half = LANES // 2
    lane = lane_mask(height)
    for k in range(layers):
        a, b = col_a[k], col_b[k]
        right = jnp.where(cp == 0, a, b)
        left = jnp.where(cp == 0, b, a)
        parts = (
            jnp.where(lane < half, right, pltpu.roll(left, half, 1)),
            jnp.where(lane < half, pltpu.roll(right, half, 1), left),
        )
        for q in range(2):
            tile3[k, q] = parts[q]
            store_by(rp, corner_a, corner_b, (k, q), parts[q][height - half :], parts[q][:half])


def read_windows(offs, obj, tile3, row_a, row_b, corner_a, corner_b, pad, win):
    rp = parity("row")
    layers, _, height, width = obj.shape
    extent = win.shape[-1] // 2
    half = extent // 2
    place_a = pl.multiple_of(jnp.where(rp == 0, height + half, 0), half)
    place_b = pl.multiple_of(jnp.where(rp == 0, 0, height + half), half)
    lane = lane_mask(extent)
    positions = offs.shape[2]
    for k in range(layers):
        for q in range(2):
            for t in range(2):
                cols = slice(t * LANES, (t + 1) * LANES)
                pad[k, q, t, pl.ds(half, height), :] = obj[k, q, :, cols]
                pad[k, q, t, pl.ds(place_a, half), :] = row_a[k, q, :, cols]
                pad[k, q, t, pl.ds(place_b, half), :] = row_b[k, q, :, cols]
            pad[k, q, 2, pl.ds(half, height), :] = tile3[k, q]
            pad[k, q, 2, pl.ds(place_a, half), :] = corner_a[k, q]
            pad[k, q, 2, pl.ds(place_b, half), :] = corner_b[k, q]
    for p in range(positions):
        tile, after, shift = col_place(offs, p, extent)
        top = offs[0, 0, p, 0]
        back = jnp.where(shift == 0, 0, LANES - shift)
        keep = lane >= shift
        for k in range(layers):
            for q in range(2):
                here = pad[k, q, tile, pl.ds(top, extent), :]
                there = pad[k, q, after, pl.ds(top, extent), :]
                joined = pltpu.roll(jnp.where(keep, here, there), back, 1)
                win[k, p * extent : (p + 1) * extent, q * extent : (q + 1) * extent] = joined


def deposit(offs, k, p, grad, acc):
    extent = grad.shape[0]
    tile, after, shift = col_place(offs, p, extent)
    top = offs[0, 0, p, 0]
    keep = lane_mask(extent) >= shift
    for q in range(2):
        moved = pltpu.roll(grad[:, q * extent : (q + 1) * extent], shift, 1)
        acc[k, q, tile, pl.ds(top, extent), :] += jnp.where(keep, moved, 0.0)
        acc[k, q, after, pl.ds(top, extent), :] += jnp.where(keep, 0.0, moved)


def forward_kernel(offs, tab, obj, tile3, row_a, row_b, corner_a, corner_b, psi_in, win, psi, psi_out, pad):
    read_windows(offs, obj, tile3, row_a, row_b, corner_a, corner_b, pad, win)
    layers = obj.shape[0]
    pairs = win.shape[1] // (2 * LANES)
    for g in range(pairs):
        rows = slice(g * 2 * LANES, (g + 1) * 2 * LANES)
        field = psi_in[rows, :]
        for k in range(layers):
            psi[k, rows, :] = field
            field = sandwich(cmul(field, win[k, rows, :]), tab, 0, False)
        psi_out[rows, :] = field


def backward_steps(offs, tab, g, field, order, psi, win, acc, last):
    rows = slice(g * 2 * LANES, (g + 1) * 2 * LANES)
    for k in order:
        grad = cmul(psi[k, rows, :], field, True)
        for i in range(2):
            deposit(offs, k, 2 * g + i, grad[i * LANES : (i + 1) * LANES], acc)
        field = cmul(win[k, rows, :], field, True)
        if not (last and k == 0):
            field = sandwich(field, tab, 0, True)
    return field


def emit_strips(acc, main, tile3, row_a, row_b, corner_a, corner_b):
    rp = parity("row")
    layers = acc.shape[0]
    height = main.shape[2]
    half = LANES // 2
    low, high = slice(0, half), slice(height + half, height + 2 * half)
    for k in range(layers):
        for q in range(2):
            for t in range(2):
                main[k, q, :, t * LANES : (t + 1) * LANES] = acc[k, q, t, half : height + half, :]
                index = (k, q, slice(None), slice(t * LANES, (t + 1) * LANES))
                store_by(rp, row_a, row_b, index, acc[k, q, t, high, :], acc[k, q, t, low, :])
            tile3[k, q] = acc[k, q, 2, half : height + half, :]
            store_by(rp, corner_a, corner_b, (k, q), acc[k, q, 2, high, :], acc[k, q, 2, low, :])


def middle_kernel(
    offs, flags, tab, obj, tile3, row_a, row_b, corner_a, corner_b, psi_in, seen,
    main, tile3_g, row_ag, row_bg, corner_ag, corner_bg, field_out,
    pad, win, psi, acc,
):
    read_windows(offs, obj, tile3, row_a, row_b, corner_a, corner_b, pad, win)
    layers = obj.shape[0]
    pairs = win.shape[1] // (2 * LANES)
    acc[...] = jnp.zeros_like(acc)
    for g in range(pairs):
        rows = slice(g * 2 * LANES, (g + 1) * 2 * LANES)
        field = psi_in[rows, :]
        for k in range(layers):
            psi[k, rows, :] = field
            field = cmul(field, win[k, rows, :])
            if k + 1 < layers:
                field = sandwich(field, tab, 0, False)
        far = sandwich(field, tab, 4, False)
        parts = []
        for i in range(2):
            p = 2 * g + i
            re = far[i * LANES : (i + 1) * LANES, :LANES]
            im = far[i * LANES : (i + 1) * LANES, LANES:]
            excess = flags[0, 0, p].astype(f32) * (re * re + im * im - seen[0, 0, p])
            parts.append(jnp.concatenate([excess * re, excess * im], axis=1))
        field = sandwich(jnp.concatenate(parts, axis=0), tab, 4, True)
        field = backward_steps(offs, tab, g, field, range(layers - 1, -1, -1), psi, win, acc, False)
        field_out[rows, :] = field
    emit_strips(acc, main, tile3_g, row_ag, row_bg, corner_ag, corner_bg)


def backward_kernel(
    offs, tab, field_in, psi, win,
    main, tile3_g, row_ag, row_bg, corner_ag, corner_bg, probe_out,
    acc,
):
    layers = psi.shape[0]
    pairs = win.shape[1] // (2 * LANES)
    acc[...] = jnp.zeros_like(acc)
    total = None
    for g in range(pairs):
        rows = slice(g * 2 * LANES, (g + 1) * 2 * LANES)
        field = backward_steps(offs, tab, g, field_in[rows, :], range(layers - 1, -1, -1), psi, win, acc, True)
        both = field[:LANES] + field[LANES:]
        total = both if total is None else total + both
    probe_out[0] = total[:, :LANES]
    probe_out[1] = total[:, LANES:]
    emit_strips(acc, main, tile3_g, row_ag, row_bg, corner_ag, corner_bg)


def col_pack_kernel(tile3, corner_a, corner_b, col_a, col_b):
    cp, rp = parity("col"), parity("row")
    layers, _, height, _ = tile3.shape
    half = LANES // 2
    lane = lane_mask(height)
    for k in range(layers):
        full = []
        for q in range(2):
            a, b = corner_a[k, q], corner_b[k, q]
            low = jnp.where(rp == 0, b, a)
            high = jnp.where(rp == 0, a, b)
            x = tile3[k, q]
            full.append(
                jnp.concatenate([x[:half] + low, x[half : height - half], x[height - half :] + high], axis=0)
            )
        right = jnp.where(lane < half, full[0], pltpu.roll(full[1], half, 1))
        left = jnp.where(lane < half, pltpu.roll(full[0], half, 1), full[1])
        store_by(cp, col_a, col_b, k, right, left)


def final_kernel(obj, main, row_a, row_b, col_a, col_b, out):
    cp, rp = parity("col"), parity("row")
    layers, _, height, width = obj.shape
    half = LANES // 2
    lane = lane_mask(height)
    for k in range(layers):
        a, b = col_a[k], col_b[k]
        from_right = jnp.where(cp == 0, a, b)
        from_left = jnp.where(cp == 0, b, a)
        for q in range(2):
            low_add = jnp.where(lane < half, from_left if q == 0 else pltpu.roll(from_left, half, 1), 0.0)
            high_add = jnp.where(lane < half, 0.0, from_right if q == 1 else pltpu.roll(from_right, half, 1))
            for t, add in ((0, low_add), (1, high_add)):
                cols = slice(t * LANES, (t + 1) * LANES)
                ra, rb = row_a[k, q, :, cols], row_b[k, q, :, cols]
                low = jnp.where(rp == 0, rb, ra)
                high = jnp.where(rp == 0, ra, rb)
                g = main[k, q, :, cols] + add
                base = obj[k, q, :, cols]
                out[k, q, :half, cols] = base[:half] - object_step * (g[:half] + low)
                out[k, q, half : height - half, cols] = (
                    base[half : height - half] - object_step * g[half : height - half]
                )
                out[k, q, height - half :, cols] = base[height - half :] - object_step * (
                    g[height - half :] + high
                )


def partner(axis, odd):
    count = lax.axis_size(axis)
    if odd:
        return [(i, (i + 1) % count if i % 2 else (i - 1) % count) for i in range(count)]
    return [(i, i ^ 1) for i in range(count)]


def pair_swap(array, axis, odd):
    return lax.ppermute(array, axis, partner(axis, odd))


def total_over(array, axes):
    for axis in axes:
        count = lax.axis_size(axis)
        step = 1
        while step < count:
            array = array + lax.ppermute(array, axis, [(i, i ^ step) for i in range(count)])
            step *= 2
    return array


def shaped(*shape, dtype=f32):
    return jax.ShapeDtypeStruct(shape, dtype)


def call(kernel, outs, ins, scratch=(), specs=None):
    return pl.pallas_call(
        kernel,
        out_shape=outs,
        in_specs=specs or [VM] * len(ins),
        out_specs=[VM] * len(outs),
        scratch_shapes=list(scratch),
        compiler_params=PARAMS,
    )(*ins)


def body(object_slices, probe_wave, offsets, active_flags, intensity, tab, chunk):
    extent = probe_wave.shape[-1]
    layers, _, height, width = object_slices.shape
    positions = offsets.shape[2]
    half = extent // 2
    rows = positions * extent
    n = chunk
    starts = list(range(0, layers, n))
    objs = [object_slices[k : k + n] for k in starts]

    def strips():
        return [shaped(n, height, LANES)] * 2 + [shaped(n, 2, half, width)] * 2

    cols, rims = [], []
    for obj in objs:
        col_a, col_b, row_a, row_b = call(pack_kernel, strips(), [obj])
        cols.append((pair_swap(col_a, "col", False), pair_swap(col_b, "col", True)))
        rims.append((pair_swap(row_a, "row", False), pair_swap(row_b, "row", True)))

    psi = jnp.concatenate([probe_wave[0], probe_wave[1]], axis=1)
    psi = jnp.concatenate([psi] * positions, axis=0)
    pad = pltpu.VMEM((n, 2, 3, height + extent, LANES), f32)
    fields = shaped(n, rows, 2 * extent)
    one = shaped(rows, 2 * extent)
    grads_out = [
        shaped(n, 2, height, width),
        shaped(n, 2, height, LANES),
        shaped(n, 2, half, width),
        shaped(n, 2, half, width),
        shaped(n, 2, half, LANES),
        shaped(n, 2, half, LANES),
    ]
    kept = []
    for i in range(len(starts)):
        tile3, corner_a, corner_b = call(
            unpack_kernel,
            [shaped(n, 2, height, LANES), shaped(n, 2, half, LANES), shaped(n, 2, half, LANES)],
            list(cols[i]),
        )
        corner_a = pair_swap(corner_a, "row", False)
        corner_b = pair_swap(corner_b, "row", True)
        ins = [objs[i], tile3, *rims[i], corner_a, corner_b, psi]
        if i + 1 < len(starts):
            win, inc, psi = call(
                forward_kernel, [fields, fields, one], [offsets, tab, *ins], [pad], [SM] + [VM] * (len(ins) + 1)
            )
            kept.append((inc, win))
        else:
            *grads, field = call(
                middle_kernel,
                grads_out + [one],
                [offsets, active_flags, tab, *ins, intensity],
                [pad, pltpu.VMEM(fields.shape, f32), pltpu.VMEM(fields.shape, f32), pad],
                [SM, SM] + [VM] * (len(ins) + 2),
            )
    updated = [None] * len(starts)
    probe_grad = None

    def send(grads):
        main, tile3, row_a, row_b, corner_a, corner_b = grads
        corner_a = pair_swap(corner_a, "row", False)
        corner_b = pair_swap(corner_b, "row", True)
        col_a, col_b = call(col_pack_kernel, [shaped(n, height, LANES)] * 2, [tile3, corner_a, corner_b])
        return (
            main,
            pair_swap(row_a, "row", False),
            pair_swap(row_b, "row", True),
            pair_swap(col_a, "col", False),
            pair_swap(col_b, "col", True),
        )

    sent = [None] * len(starts)
    sent[-1] = send(grads)
    for i in range(len(starts) - 2, -1, -1):
        inc, win = kept[i]
        *grads, field = call(
            backward_kernel,
            grads_out + [shaped(2, extent, extent)],
            [offsets, tab, field, inc, win],
            [pad],
            [SM] + [VM] * 4,
        )
        sent[i] = send(grads)
    for i in range(len(starts)):
        (updated[i],) = call(final_kernel, [shaped(n, 2, height, width)], [objs[i], *sent[i]])
    updated_object = jnp.concatenate(updated, axis=0)
    devices = lax.axis_size("row") * lax.axis_size("col")
    factor = 1.0 / math.sqrt(positions * devices)
    updated_probe = probe_wave - factor * total_over(field, ("row", "col"))
    return (updated_object, updated_probe)


def solution(mesh):
    in_specs = (
        P(None, None, "row", "col"),
        P(),
        P("row", "col", None, None),
        P("row", "col", None),
        P("row", "col", None, None, None),
        P(),
    )
    out_specs = (P(None, None, "row", "col"), P())

    def run(object_slices, probe_wave, offsets, active_flags, intensity):
        tab = jnp.asarray(tables_np(probe_wave.shape[-1]))
        step = jax.shard_map(
            functools.partial(body, chunk=2), mesh=mesh, in_specs=in_specs, out_specs=out_specs, check_vma=False
        )
        return step(object_slices, probe_wave, offsets, active_flags, intensity, tab)

    return run
```
